32 devices in a mesh: dp: 2 (over x), seq: 16 (over z, y, core).
Axes of the slice: x: 2, y: 2, z: 4, core: 2. Of those that a mesh axis runs over, the one named last changes fastest.
Arguments:
- queries: bfloat16 [16384, 1024], P(('dp', 'seq')), parts along dimension 0, may hold values from -6 to 6
- keys: bfloat16 [16384, 1024], P(('dp', 'seq')), parts along dimension 0, may hold values from -6 to 6
- values: bfloat16 [16384, 1024], P(('dp', 'seq')), parts along dimension 0, may hold values from -6 to 6
- out_grad: bfloat16 [16384, 1024], P(('dp', 'seq')), parts along dimension 0, may hold values from -6 to 6
- pattern: int32 [256, 4], P(('dp', 'seq')), parts along dimension 0, may hold values from -16 to 16, as said below
Outputs:
- attended: bfloat16 [16384, 1024], P(('dp', 'seq')), parts along dimension 0
- query_grad: bfloat16 [16384, 1024], P(('dp', 'seq')), parts along dimension 0
- key_grad: bfloat16 [16384, 1024], P(('dp', 'seq')), parts along dimension 0
- value_grad: bfloat16 [16384, 1024], P(('dp', 'seq')), parts along dimension 0
The draws below stay inside these ranges and needn't reach their ends.
There are 2 independent parts, one for each index of `dp`. The reference program is written for one: setup_inputs(seed, part) draws one part's arguments, and reference() takes and returns one part's arrays. A program takes and returns all parts, laid end to end along the dimension named above; each array names one. Nothing has to cross between parts.
Inputs may be any that keep to these rules, and one draw needn't show every extreme that they name: pattern[b, c] has magnitude between 3 and 16; offsets of one block may repeat; pattern[b, 0] is 16 where b % 8 == 0 and -16 where b % 8 == 1.
All inputs are finite; a program needn't handle non-finite values.
Results may differ from the reference program's by a relative error of at most 0.02.
Values may be sent and summed in bfloat16 or wider, within the bound.
A program may use at most 512 MiB of HBM per device.

```python
import jax
import jax.numpy as jnp
from jax import lax

HEADS = 16
HEAD = 64
D = 1024
QB = 64
TOK_DEV = 512
BLK_DEV = 8
TOKENS = 8192
BLOCKS = 128
N_SEQ = 16


def paired_draw(key):
    base = jax.random.fold_in(key, 5)
    first, second = jax.random.split(base, 2)
    query_vals = jax.random.truncated_normal(first, -6.0, 6.0, (TOKENS, D), jnp.float32)
    key_vals = jax.random.truncated_normal(second, -6.0, 6.0, (TOKENS, D), jnp.float32)
    return (query_vals.astype(jnp.bfloat16), key_vals.astype(jnp.bfloat16))


def draw_queries(key, part):
    return paired_draw(key)[0]


def draw_keys(key, part):
    return paired_draw(key)[1]


def draw_pattern(key, part):
    mag_key, sign_key = jax.random.split(jax.random.fold_in(key, 11))
    magnitude = jax.random.randint(mag_key, (BLOCKS, 4), 3, 2 * BLK_DEV + 1, dtype=jnp.int32)
    signs = jax.random.randint(sign_key, (BLOCKS, 4), 0, 2, dtype=jnp.int32) * 2 - 1
    offsets = magnitude * signs
    rows = (jnp.arange(BLOCKS, dtype=jnp.int32) % BLK_DEV)[:, None]
    column = jnp.arange(4, dtype=jnp.int32)[None, :]
    offsets = jnp.where((rows == 0) & (column == 0), 2 * BLK_DEV, offsets)
    offsets = jnp.where((rows == 1) & (column == 0), -2 * BLK_DEV, offsets)
    return offsets.astype(jnp.int32)


def level_of(key, shape, cuts, smallest, high):
    gain, own = 1.0, jax.random.fold_in(key, 6)
    for axis_at, parts in cuts:
        heights = jnp.exp(jax.random.uniform(jax.random.fold_in(own, axis_at), (parts,), jnp.float32, smallest / len(cuts), high / len(cuts)))
        gain = gain * jnp.repeat(heights, shape[axis_at] // parts).reshape([-1 if axis == axis_at else 1 for axis in range(len(shape))])
    return gain


def bell_draw(own_key, dims, deviation, bound, pieces=(), kind=jnp.bfloat16):
    drawn = deviation * jax.random.normal(own_key, dims, jnp.float32)
    if pieces:
        drawn = drawn * level_of(own_key, dims, pieces, -0.22, 0.18)
    return jnp.clip(drawn, -bound, bound).astype(kind)


def setup_inputs(seed: int = 0, part: int = 0) -> dict:
    key_list = jax.random.split(jax.random.key(seed), 6)
    part_keys = jax.random.split(jax.random.fold_in(key_list[5], part), 6)
    return {
        "queries": draw_queries(jax.random.fold_in(jax.random.fold_in(key_list[5], part), 71), part),
        "keys": draw_keys(jax.random.fold_in(jax.random.fold_in(key_list[5], part), 71), part),
        "values": bell_draw(part_keys[2], (TOKENS, D), 1.0, 6.0, ((0, 16),)),
        "out_grad": bell_draw(part_keys[3], (TOKENS, D), 1.0, 6.0, ((0, 16),)),
        "pattern": draw_pattern(jax.random.fold_in(jax.random.fold_in(key_list[5], part), 71), part),
    }


def allowed_slots(usable):
    slot_index = jnp.arange(8 * QB, dtype=jnp.int32)
    slot_block = slot_index // QB
    within = slot_index % QB
    query_pos = jnp.arange(QB, dtype=jnp.int32)
    nearby = (slot_block[None, :] != 0) | (within[None, :] >= query_pos[:, None])
    key_usable = jnp.repeat(usable, QB, axis=1)
    return nearby[None, :, :] & key_usable[:, None, :]


def attend_group(query_part, keys_near, values_near, grad_part, allowed):
    score_scale = HEAD ** -0.5
    query_wide = query_part.astype(jnp.float32)
    keys_wide = keys_near.astype(jnp.float32)
    values_wide = values_near.astype(jnp.float32)
    grad_wide = grad_part.astype(jnp.float32)
    scores = jnp.einsum('bqhe,bkhe->bhqk', query_wide, keys_wide) * score_scale
    scores = jnp.where(allowed[:, None, :, :], scores, -1e30)
    row_max = jnp.max(scores, axis=-1, keepdims=True)
    lifted = jnp.exp(scores - row_max)
    softmax = lifted / jnp.sum(lifted, axis=-1, keepdims=True)
    softmax_low = softmax.astype(jnp.bfloat16)
    attended = jnp.einsum('bhqk,bkhe->bqhe', softmax_low.astype(jnp.float32), values_wide).astype(jnp.bfloat16)
    row_dots = jnp.sum(grad_wide * attended.astype(jnp.float32), axis=-1)
    grad_probs = jnp.einsum('bqhe,bkhe->bhqk', grad_wide, values_wide)
    grad_scores = (softmax * (grad_probs - jnp.transpose(row_dots, (0, 2, 1))[..., None])).astype(jnp.bfloat16)
    grad_scores_wide = grad_scores.astype(jnp.float32)
    query_grad = (jnp.einsum('bhqk,bkhe->bqhe', grad_scores_wide, keys_wide) * score_scale).astype(jnp.bfloat16)
    key_terms = jnp.einsum('bhqk,bqhe->bkhe', grad_scores_wide, query_wide) * score_scale
    value_terms = jnp.einsum('bhqk,bqhe->bkhe', softmax_low.astype(jnp.float32), grad_wide)
    return attended, query_grad, key_terms, value_terms


def reference(queries, keys, values, out_grad, pattern):
    reach = 2 * BLK_DEV
    joined = jnp.concatenate([keys, values], axis=1)
    border = jnp.zeros((reach * QB, 2 * D), jnp.bfloat16)
    padded_blocks = jnp.concatenate([border, joined, border], axis=0).reshape(BLOCKS + 2 * reach, QB, 2 * D)
    window = jnp.broadcast_to(jnp.array([-2, -1, 0, 1], dtype=jnp.int32), (BLK_DEV, 4))

    def advance(totals, shard_index):
        first_block = shard_index * BLK_DEV
        local_blocks = (first_block + jnp.arange(BLK_DEV, dtype=jnp.int32))[:, None]
        query_rows = lax.dynamic_slice_in_dim(queries, shard_index * TOK_DEV, TOK_DEV, 0)
        grad_rows = lax.dynamic_slice_in_dim(out_grad, shard_index * TOK_DEV, TOK_DEV, 0)
        pattern_rows = lax.dynamic_slice_in_dim(pattern, first_block, BLK_DEV, 0).astype(jnp.int32)
        offsets = jnp.concatenate([window, pattern_rows], axis=1)
        target = local_blocks + offsets
        usable = (target >= 0) & (target < BLOCKS)
        key_slots = (target + reach).astype(jnp.int32)
        gathered = jnp.take(padded_blocks, key_slots, axis=0)
        keys_near = gathered[..., :D].reshape(BLK_DEV, 8 * QB, HEADS, HEAD)
        values_near = gathered[..., D:].reshape(BLK_DEV, 8 * QB, HEADS, HEAD)
        attended, query_grad, key_terms, value_terms = attend_group(
            query_rows.reshape(BLK_DEV, QB, HEADS, HEAD), keys_near, values_near,
            grad_rows.reshape(BLK_DEV, QB, HEADS, HEAD), allowed_slots(usable))
        terms = jnp.concatenate([key_terms.reshape(BLK_DEV, 8, QB, D), value_terms.reshape(BLK_DEV, 8, QB, D)], axis=-1)
        totals = totals.at[key_slots].add(terms)
        return totals, (attended.reshape(TOK_DEV, D), query_grad.reshape(TOK_DEV, D))

    start_totals = jnp.zeros((BLOCKS + 2 * reach, QB, 2 * D), jnp.float32)
    totals, (attended, query_grad) = lax.scan(advance, start_totals, jnp.arange(N_SEQ, dtype=jnp.int32))
    grads = totals[reach:reach + BLOCKS].reshape(TOKENS, 2 * D)
    return (attended.reshape(TOKENS, D), query_grad.reshape(TOKENS, D),
            grads[:, :D].astype(jnp.bfloat16), grads[:, D:].astype(jnp.bfloat16))
```

```python
import jax
import jax.numpy as jnp
from jax import lax
from jax.experimental import pallas as pl
from jax.experimental.pallas import tpu as pltpu
from jax.sharding import PartitionSpec as P

HEAD = 64
QB = 64
GROUP = 4
PHASES = 1
NEG = -1e30
SCALE = HEAD ** (-0.5)


def diag_rows(block, heads):
    tiled = jnp.concatenate([block] * heads, axis=0)
    row = lax.broadcasted_iota(jnp.int32, tiled.shape, 0) // QB
    col = lax.broadcasted_iota(jnp.int32, tiled.shape, 1) // HEAD
    return jnp.where(row == col, tiled, jnp.zeros_like(tiled))


def diag_pick(full, heads):
    col = lax.broadcasted_iota(jnp.int32, (QB, heads * HEAD), 1) // HEAD
    out = full[:QB]
    for h in range(1, heads):
        out = jnp.where(col == h, full[h * QB : (h + 1) * QB], out)
    return out


def attend_kernel(
    slot_ref, usable_ref, q_ref, g_ref, k_ref, v_ref,
    att_ref, dq_ref, dk_own_ref, dv_own_ref, dk_far_ref, dv_far_ref,
    dk_acc, dv_acc, *, reach, own,
):
    i = pl.program_id(0)
    width = q_ref.shape[-1]
    heads = width // HEAD

    @pl.when(i == 0)
    def _():
        dk_acc[...] = jnp.zeros_like(dk_acc)
        dv_acc[...] = jnp.zeros_like(dv_acc)

    slots = [slot_ref[i, s] for s in range(8)]
    q_bd = diag_rows(q_ref[...], heads)
    g_bd = diag_rows(g_ref[...], heads)
    keys = jnp.concatenate([k_ref[t] for t in slots], axis=0)
    vals = jnp.concatenate([v_ref[t] for t in slots], axis=0)
    nt = (((1,), (1,)), ((), ()))
    tn = (((0,), (0,)), ((), ()))
    f32 = jnp.float32
    scores = lax.dot_general(keys, q_bd, nt, preferred_element_type=f32) * SCALE
    parts = []
    for s in range(8):
        part = scores[s * QB : (s + 1) * QB]
        bias = jnp.where(usable_ref[i, s] != 0, 0.0, NEG).astype(f32)
        part = part + bias
        if s == 0:
            within = lax.broadcasted_iota(jnp.int32, part.shape, 0)
            pos = lax.broadcasted_iota(jnp.int32, part.shape, 1) % QB
            part = jnp.where(within >= pos, part, NEG)
        parts.append(part)
    scores = jnp.concatenate(parts, axis=0)
    top = jnp.max(scores, axis=0, keepdims=True)
    lifted = jnp.exp(scores - top)
    total = jnp.sum(lifted, axis=0, keepdims=True)
    inv = 1.0 / total
    probs = lifted * inv
    probs_low = probs.astype(jnp.bfloat16)
    grad_probs = lax.dot_general(vals, g_bd, nt, preferred_element_type=f32)
    dots = jnp.sum(probs * grad_probs, axis=0, keepdims=True)
    ds = (probs * (grad_probs - dots)).astype(jnp.bfloat16)
    att = lax.dot_general(probs_low, vals, tn, preferred_element_type=f32)
    att_ref[...] = diag_pick(att, heads).astype(jnp.bfloat16)
    dq = lax.dot_general(ds, keys, tn, preferred_element_type=f32)
    dq_ref[...] = (diag_pick(dq, heads) * SCALE).astype(jnp.bfloat16)
    dk = jnp.dot(ds, q_bd, preferred_element_type=f32)
    dv = jnp.dot(probs_low, g_bd, preferred_element_type=f32)
    for s in range(8):
        dk_acc[slots[s]] += dk[s * QB : (s + 1) * QB]
        dv_acc[slots[s]] += dv[s * QB : (s + 1) * QB]

    @pl.when(i == pl.num_programs(0) - 1)
    def _():
        dk_own_ref[...] = dk_acc[reach : reach + own] * SCALE
        dv_own_ref[...] = dv_acc[reach : reach + own]
        for acc, ref, scale in ((dk_acc, dk_far_ref, SCALE), (dv_acc, dv_far_ref, 1.0)):
            ref[:reach] = (acc[:reach] * scale).astype(jnp.bfloat16)
            ref[reach:] = (acc[reach + own :] * scale).astype(jnp.bfloat16)


def attend(slots, usable, q, g, k_win, v_win, reach, own):
    width = q.shape[-1]
    win = own + 2 * reach
    bf16 = jnp.bfloat16
    row = pl.BlockSpec((QB, width), lambda i, *_: (i, 0))

    def whole(n):
        return pl.BlockSpec((n, QB, width), lambda i, *_: (0, 0, 0))

    import functools

    return pl.pallas_call(
        functools.partial(attend_kernel, reach=reach, own=own),
        grid_spec=pltpu.PrefetchScalarGridSpec(
            num_scalar_prefetch=2,
            grid=(own,),
            in_specs=[row, row, whole(win), whole(win)],
            out_specs=[row, row, whole(own), whole(own), whole(2 * reach), whole(2 * reach)],
            scratch_shapes=[
                pltpu.VMEM((win, QB, width), jnp.float32),
                pltpu.VMEM((win, QB, width), jnp.float32),
            ],
        ),
        out_shape=[
            jax.ShapeDtypeStruct(q.shape, bf16),
            jax.ShapeDtypeStruct(q.shape, bf16),
            jax.ShapeDtypeStruct((own, QB, width), jnp.float32),
            jax.ShapeDtypeStruct((own, QB, width), jnp.float32),
            jax.ShapeDtypeStruct((2 * reach, QB, width), bf16),
            jax.ShapeDtypeStruct((2 * reach, QB, width), bf16),
        ],
        compiler_params=pltpu.CompilerParams(dimension_semantics=("arbitrary",)),
        name="attend",
    )(slots, usable, q, g, k_win, v_win)


def trade(pieces_of, count, me):
    member = me % GROUP
    mine = pieces_of(member)
    out = jnp.zeros((GROUP,) + mine.shape, mine.dtype)
    out = lax.dynamic_update_index_in_dim(out, mine, member, 0)
    for d in range(1, GROUP):
        got = lax.ppermute(pieces_of(member ^ d), "seq", [(s, s ^ d) for s in range(count)])
        out = lax.dynamic_update_index_in_dim(out, got, member ^ d, 0)
    return out


def hop(value, count, step):
    pairs = [(s, s + step) for s in range(max(0, -step), min(count, count - step))]
    return lax.ppermute(value, "seq", pairs)


def on_device(queries, keys, values, out_grad, pattern):
    tokens, model = queries.shape
    blocks = tokens // QB
    count = lax.axis_size("seq")
    me = lax.axis_index("seq")
    cols = model // GROUP
    width = cols // PHASES
    reach = 2 * blocks
    own = GROUP * blocks
    win = own + 2 * reach
    level_tokens = GROUP * tokens
    far = reach * QB

    level_pattern = lax.all_gather(
        pattern, "seq", axis_index_groups=[list(range(s, s + GROUP)) for s in range(0, count, GROUP)]
    ).reshape(own, 4)
    local = jnp.arange(own, dtype=jnp.int32)[:, None]
    near = jnp.broadcast_to(jnp.array([-2, -1, 0, 1], dtype=jnp.int32), (own, 4))
    target = local + jnp.concatenate([near, level_pattern], axis=1)
    slots = target + reach
    target = target + (me // GROUP) * own
    usable = ((target >= 0) & (target < count * blocks)).astype(jnp.int32)

    outs = []
    for phase in range(PHASES):

        def cut(arrays, phase=phase):
            def piece(t):
                start = t * cols + phase * width
                return jnp.stack([lax.dynamic_slice_in_dim(a, start, width, 1) for a in arrays])

            return piece

        kv = trade(cut((keys, values)), count, me)
        qg = trade(cut((queries, out_grad)), count, me)
        kv = jnp.swapaxes(kv, 0, 1).reshape(2, level_tokens, width)
        qg = jnp.swapaxes(qg, 0, 1).reshape(2, level_tokens, width)
        before = hop(kv[:, level_tokens - far :], count, GROUP)
        after = hop(kv[:, :far], count, -GROUP)
        kv_win = jnp.concatenate([before, kv, after], axis=1).reshape(2, win, QB, width)
        att, dq, dk_own, dv_own, dk_far, dv_far = attend(
            slots, usable, qg[0], qg[1], kv_win[0], kv_win[1], reach, own
        )
        far_grads = jnp.stack([dk_far, dv_far]).reshape(2, 2 * far, width)
        from_after = hop(far_grads[:, :far], count, -GROUP)
        from_before = hop(far_grads[:, far:], count, GROUP)
        own_grads = jnp.stack([dk_own, dv_own]).reshape(2, level_tokens, width)
        add = jnp.concatenate(
            [
                from_before,
                jnp.zeros((2, level_tokens - 2 * far, width), from_before.dtype),
                from_after,
            ],
            axis=1,
        )
        grads = (own_grads + add.astype(jnp.float32)).astype(jnp.bfloat16)

        def rows(stacked):
            return lambda t: lax.dynamic_slice_in_dim(stacked, t * tokens, tokens, 1)

        outs.append(
            (
                trade(rows(jnp.stack([att, dq])), count, me),
                trade(rows(grads), count, me),
            )
        )
    result = []
    for which in range(2):
        full = jnp.stack([o[which] for o in outs])
        full = jnp.transpose(full, (2, 3, 1, 0, 4)).reshape(2, tokens, model)
        result += [full[0], full[1]]
    return tuple(result)


def solution(mesh):
    spec = P(("dp", "seq"), None)
    return jax.shard_map(
        on_device,
        mesh=mesh,
        in_specs=(spec,) * 5,
        out_specs=(spec,) * 4,
        check_vma=False,
    )
```

```python
import functools

import jax
import jax.numpy as jnp
from jax import lax
from jax.experimental import pallas as pl
from jax.experimental.pallas import tpu as pltpu
from jax.sharding import PartitionSpec as P

HEAD = 64
QB = 64
GROUP = 4
PHASES = 2
NEG = -1e30
SCALE = HEAD ** (-0.5)


def diag_rows(block, heads):
    tiled = jnp.concatenate([block] * heads, axis=0)
    row = lax.broadcasted_iota(jnp.int32, tiled.shape, 0) // QB
    col = lax.broadcasted_iota(jnp.int32, tiled.shape, 1) // HEAD
    return jnp.where(row == col, tiled, jnp.zeros_like(tiled))


def diag_pick(full, heads):
    col = lax.broadcasted_iota(jnp.int32, (QB, heads * HEAD), 1) // HEAD
    out = full[:QB]
    for h in range(1, heads):
        out = jnp.where(col == h, full[h * QB : (h + 1) * QB], out)
    return out


def attend_kernel(*refs, reach, shard):
    slot_ref, usable_ref = refs[:2]
    kv_pieces, kv_far, qg_pieces = refs[2 : 2 + GROUP], refs[2 + GROUP : 4 + GROUP], refs[4 + GROUP : 4 + 2 * GROUP]
    attdq_ref, own_ref, far_ref, kv_win, qg_win, dk_acc, dv_acc, sems = refs[4 + 2 * GROUP :]
    i = pl.program_id(0)
    width = kv_win.shape[-1]
    heads = width // HEAD
    own = GROUP * shard

    @pl.when(i == 0)
    def _():
        copies = []

        def bring(src, dst):
            copy = pltpu.make_async_copy(src, dst, sems.at[len(copies)])
            copy.start()
            copies.append(copy)

        for d in range(GROUP):
            bring(kv_pieces[d], kv_win.at[:, reach + d * shard : reach + (d + 1) * shard])
            bring(qg_pieces[d], qg_win.at[:, d * shard : (d + 1) * shard])
        for side, base in enumerate((0, reach + own)):
            for e in range(2):
                start = base + e * shard
                bring(kv_far[side].at[e], kv_win.at[:, start : start + shard])
        dk_acc[...] = jnp.zeros_like(dk_acc)
        dv_acc[...] = jnp.zeros_like(dv_acc)
        for copy in copies:
            copy.wait()

    slots = [slot_ref[i, s] for s in range(8)]
    q_bd = diag_rows(qg_win[0, i], heads)
    g_bd = diag_rows(qg_win[1, i], heads)
    keys = jnp.concatenate([kv_win[0, t] for t in slots], axis=0)
    vals = jnp.concatenate([kv_win[1, t] for t in slots], axis=0)
    nt = (((1,), (1,)), ((), ()))
    tn = (((0,), (0,)), ((), ()))
    f32 = jnp.float32
    scores = lax.dot_general(keys, q_bd, nt, preferred_element_type=f32) * SCALE
    parts = []
    for s in range(8):
        part = scores[s * QB : (s + 1) * QB]
        bias = jnp.where(usable_ref[i, s] != 0, 0.0, NEG).astype(f32)
        part = part + bias
        if s == 0:
            within = lax.broadcasted_iota(jnp.int32, part.shape, 0)
            pos = lax.broadcasted_iota(jnp.int32, part.shape, 1) % QB
            part = jnp.where(within >= pos, part, NEG)
        parts.append(part)
    scores = jnp.concatenate(parts, axis=0)
    top = jnp.max(scores, axis=0, keepdims=True)
    lifted = jnp.exp(scores - top)
    total = jnp.sum(lifted, axis=0, keepdims=True)
    inv = 1.0 / total
    probs = lifted * inv
    probs_low = probs.astype(jnp.bfloat16)
    grad_probs = lax.dot_general(vals, g_bd, nt, preferred_element_type=f32)
    dots = jnp.sum(probs * grad_probs, axis=0, keepdims=True)
    ds = (probs * (grad_probs - dots)).astype(jnp.bfloat16)
    att = lax.dot_general(probs_low, vals, tn, preferred_element_type=f32)
    attdq_ref[0, 0] = diag_pick(att, heads).astype(jnp.bfloat16)
    dq = lax.dot_general(ds, keys, tn, preferred_element_type=f32)
    attdq_ref[0, 1] = (diag_pick(dq, heads) * SCALE).astype(jnp.bfloat16)
    dk = jnp.dot(ds, q_bd, preferred_element_type=f32)
    dv = jnp.dot(probs_low, g_bd, preferred_element_type=f32)
    for s in range(8):
        dk_acc[slots[s]] += dk[s * QB : (s + 1) * QB]
        dv_acc[slots[s]] += dv[s * QB : (s + 1) * QB]

    @pl.when(i == pl.num_programs(0) - 1)
    def _():
        for j, acc, scale in ((0, dk_acc, SCALE), (1, dv_acc, 1.0)):
            for d in range(GROUP):
                start = reach + d * shard
                own_ref[d, j] = acc[start : start + shard] * scale
            for e in range(4):
                start = e * shard if e < 2 else own + e * shard
                far_ref[e, j] = (acc[start : start + shard] * scale).astype(jnp.bfloat16)


def attend(slots, usable, kv_pieces, kv_far, qg_pieces, reach, shard):
    width = kv_pieces[0].shape[-1]
    own = GROUP * shard
    win = own + 2 * reach
    bf16, f32 = jnp.bfloat16, jnp.float32
    anywhere = pl.BlockSpec(memory_space=pl.ANY)

    def whole(n):
        return pl.BlockSpec((n, 2, shard, QB, width), lambda i, *_: (0,) * 5)

    return pl.pallas_call(
        functools.partial(attend_kernel, reach=reach, shard=shard),
        grid_spec=pltpu.PrefetchScalarGridSpec(
            num_scalar_prefetch=2,
            grid=(own,),
            in_specs=[anywhere] * (2 * GROUP + 2),
            out_specs=[
                pl.BlockSpec((1, 2, QB, width), lambda i, *_: (i // shard, 0, i % shard, 0)),
                whole(GROUP),
                whole(4),
            ],
            scratch_shapes=[
                pltpu.VMEM((2, win, QB, width), bf16),
                pltpu.VMEM((2, own, QB, width), bf16),
                pltpu.VMEM((win, QB, width), f32),
                pltpu.VMEM((win, QB, width), f32),
                pltpu.SemaphoreType.DMA((2 * GROUP + 4,)),
            ],
        ),
        out_shape=[
            jax.ShapeDtypeStruct((GROUP, 2, shard * QB, width), bf16),
            jax.ShapeDtypeStruct((GROUP, 2, shard, QB, width), f32),
            jax.ShapeDtypeStruct((4, 2, shard, QB, width), bf16),
        ],
        cost_estimate=pl.CostEstimate(
            flops=120 * own * 8 * QB * width * width, bytes_accessed=16 << 20, transcendentals=own * 8 * QB * width
        ),
        compiler_params=pltpu.CompilerParams(dimension_semantics=("arbitrary",)),
        name="attend",
    )(slots, usable, *kv_pieces, *kv_far, *qg_pieces)


def lay_kernel(member_ref, *refs):
    per = len(refs) - 4
    pieces, outs = refs[:per], refs[per:]
    width = pieces[0].shape[-1]
    member = member_ref[0]
    at = 0
    for phase in range(PHASES):
        for pair in range(2):
            for d in range(GROUP):
                piece = pieces[at]
                at += 1
                start = pl.multiple_of(((member ^ d) * PHASES + phase) * width, width)
                for j in range(2):
                    value = piece[0, j] if d == 0 else piece[j]
                    outs[2 * pair + j][:, pl.ds(start, width)] = value


def lay(member, pieces, tokens, model, rows=128):
    in_specs = []
    for n, piece in enumerate(pieces):
        width = piece.shape[-1]
        if n % GROUP == 0:
            in_specs.append(pl.BlockSpec((1, 2, rows, width), lambda r, *_: (0, 0, r, 0)))
        else:
            in_specs.append(pl.BlockSpec((2, rows, width), lambda r, *_: (0, r, 0)))
    return pl.pallas_call(
        lay_kernel,
        grid_spec=pltpu.PrefetchScalarGridSpec(
            num_scalar_prefetch=1,
            grid=(tokens // rows,),
            in_specs=in_specs,
            out_specs=[pl.BlockSpec((rows, model), lambda r, *_: (r, 0))] * 4,
        ),
        out_shape=[jax.ShapeDtypeStruct((tokens, model), jnp.bfloat16)] * 4,
        name="lay",
    )(member, *pieces)


def on_device(queries, keys, values, out_grad, pattern):
    tokens, model = queries.shape
    shard = tokens // QB
    count = lax.axis_size("seq")
    me = lax.axis_index("seq")
    member = me % GROUP
    high, low = member // 2, member % 2
    cols = model // GROUP
    width = cols // PHASES
    reach = 2 * shard
    own = GROUP * shard

    def swap(value, d):
        return lax.ppermute(value, "seq", [(s, s ^ d) for s in range(count)])

    def hop(value, step):
        pairs = [(s, s + step) for s in range(max(0, -step), min(count, count - step))]
        return lax.ppermute(value, "seq", pairs)

    level_pattern = jnp.stack([pattern] + [swap(pattern, d) for d in range(1, GROUP)])
    place = jnp.arange(GROUP, dtype=jnp.int32)[:, None]
    local = ((place ^ member) * shard + jnp.arange(shard, dtype=jnp.int32)).reshape(own, 1)
    near = jnp.broadcast_to(jnp.array([-2, -1, 0, 1], dtype=jnp.int32), (own, 4))
    target = local + jnp.concatenate([near, level_pattern.reshape(own, 4)], axis=1)
    in_shard = target % shard
    level_shard = target // shard
    inside = (level_shard >= 0) & (level_shard < GROUP)
    held = jnp.where(
        inside,
        2 + (level_shard ^ member),
        jnp.where(level_shard < 0, (level_shard + 2) ^ low, 2 + GROUP + ((level_shard - GROUP) ^ low)),
    )
    slots = held * shard + in_shard
    target = target + (me // GROUP) * own
    usable = ((target >= 0) & (target < count * shard)).astype(jnp.int32)

    def cut(arrays, d, phase):
        start = (member ^ d) * cols + phase * width
        return jnp.stack([lax.dynamic_slice_in_dim(a, start, width, 1) for a in arrays])

    def bring(arrays, phase):
        return [cut(arrays, 0, phase)] + [swap(cut(arrays, d, phase), d) for d in range(1, GROUP)]

    kvs = [bring((keys, values), phase) for phase in range(PHASES)]
    qgs = [bring((queries, out_grad), phase) for phase in range(PHASES)]
    fars = []
    for kv in kvs:
        near_pair, cross_pair = jnp.stack(kv[:2]), jnp.stack(kv[2:])
        upper = jnp.where(high == 1, near_pair, cross_pair)
        lower = jnp.where(high == 1, cross_pair, near_pair)
        fars.append((hop(upper, GROUP), hop(lower, -GROUP)))

    blocked = (2, shard, QB, width)
    pieces = []
    for phase in range(PHASES):
        attdq, own_grads, far_grads = attend(
            slots,
            usable,
            [p.reshape(blocked) for p in kvs[phase]],
            [f.reshape((2,) + blocked) for f in fars[phase]],
            [p.reshape(blocked) for p in qgs[phase]],
            reach,
            shard,
        )
        far_grads = far_grads.reshape(4, 2, tokens, width)
        own_grads = own_grads.reshape(GROUP, 2, tokens, width)
        for_upper = hop(far_grads[:2], -GROUP)
        for_lower = hop(far_grads[2:], GROUP)
        pieces += [attdq] + [swap(attdq[d], d) for d in range(1, GROUP)]
        near_add = jnp.where(high == 1, for_upper, for_lower)
        cross_add = jnp.where(high == 1, for_lower, for_upper)
        add = jnp.concatenate([near_add, cross_add]).astype(jnp.float32)
        grads = (own_grads + add).astype(jnp.bfloat16)
        pieces += [grads] + [swap(grads[d], d) for d in range(1, GROUP)]
    return tuple(lay(member.reshape(1), pieces, tokens, model))


def solution(mesh):
    spec = P(("dp", "seq"), None)
    return jax.shard_map(
        on_device,
        mesh=mesh,
        in_specs=(spec,) * 5,
        out_specs=(spec,) * 4,
        check_vma=False,
    )
```

```python
import functools

import jax
import jax.numpy as jnp
from jax import lax
from jax.experimental import pallas as pl
from jax.experimental.pallas import tpu as pltpu
from jax.sharding import PartitionSpec as P

HEAD = 64
QB = 64
GROUP = 4
PHASES = 2
UNROLL = 4
NEG = -1e30
SCALE = HEAD ** (-0.5)


def diag_rows(block, heads):
    tiled = jnp.concatenate([block] * heads, axis=0)
    row = lax.broadcasted_iota(jnp.int32, tiled.shape, 0) // QB
    col = lax.broadcasted_iota(jnp.int32, tiled.shape, 1) // HEAD
    return jnp.where(row == col, tiled, jnp.zeros_like(tiled))


def diag_pick(full, heads):
    col = lax.broadcasted_iota(jnp.int32, (QB, heads * HEAD), 1) // HEAD
    out = full[:QB]
    for h in range(1, heads):
        out = jnp.where(col == h, full[h * QB : (h + 1) * QB], out)
    return out


def attend_kernel(*refs, reach, shard):
    slot_ref, usable_ref = refs[:2]
    kv_pieces, kv_far, qg_pieces = refs[2 : 2 + GROUP], refs[2 + GROUP : 4 + GROUP], refs[4 + GROUP : 4 + 2 * GROUP]
    attdq_ref, own_ref, far_ref, kv_win, qg_win, dk_acc, dv_acc, sems = refs[4 + 2 * GROUP :]
    i = pl.program_id(0)
    width = kv_win.shape[-1]
    heads = width // HEAD
    own = GROUP * shard

    @pl.when(i == 0)
    def _():
        copies = []

        def bring(src, dst):
            copy = pltpu.make_async_copy(src, dst, sems.at[len(copies)])
            copy.start()
            copies.append(copy)

        for d in range(GROUP):
            bring(kv_pieces[d], kv_win.at[:, reach + d * shard : reach + (d + 1) * shard])
            bring(qg_pieces[d], qg_win.at[:, d * shard : (d + 1) * shard])
        for side, base in enumerate((0, reach + own)):
            for e in range(2):
                start = base + e * shard
                bring(kv_far[side].at[e], kv_win.at[:, start : start + shard])
        dk_acc[...] = jnp.zeros_like(dk_acc)
        dv_acc[...] = jnp.zeros_like(dv_acc)
        for copy in copies:
            copy.wait()

    nt = (((1,), (1,)), ((), ()))
    tn = (((0,), (0,)), ((), ()))
    f32 = jnp.float32
    every = range(UNROLL)
    blocks = [i * UNROLL + u for u in every]
    slots = [[slot_ref[b, s] for s in range(8)] for b in blocks]
    q_bd = [diag_rows(qg_win[0, b] * jnp.bfloat16(SCALE), heads) for b in blocks]
    g_bd = [diag_rows(qg_win[1, b], heads) for b in blocks]
    keys = [jnp.concatenate([kv_win[0, t] for t in slots[u]], axis=0) for u in every]
    vals = [jnp.concatenate([kv_win[1, t] for t in slots[u]], axis=0) for u in every]
    raw = [lax.dot_general(keys[u], q_bd[u], nt, preferred_element_type=f32) for u in every]
    grad_probs = [lax.dot_general(vals[u], g_bd[u], nt, preferred_element_type=f32) for u in every]
    probs_low, ds = [], []
    for u in every:
        parts = []
        for s in range(8):
            part = raw[u][s * QB : (s + 1) * QB]
            if s != 2:
                part = part + jnp.where(usable_ref[blocks[u], s] != 0, 0.0, NEG).astype(f32)
            if s == 0:
                within = lax.broadcasted_iota(jnp.int32, part.shape, 0)
                pos = lax.broadcasted_iota(jnp.int32, part.shape, 1) % QB
                part = jnp.where(within >= pos, part, NEG)
            parts.append(part)
        scores = jnp.concatenate(parts, axis=0)
        top = jnp.max(scores, axis=0, keepdims=True)
        lifted = jnp.exp(scores - top)
        inv = 1.0 / jnp.sum(lifted, axis=0, keepdims=True)
        probs = lifted * inv
        probs_low.append(probs.astype(jnp.bfloat16))
        dots = jnp.sum(probs * grad_probs[u], axis=0, keepdims=True)
        ds.append((probs * (grad_probs[u] - dots)).astype(jnp.bfloat16))
    for u in every:
        att = lax.dot_general(probs_low[u], vals[u], tn, preferred_element_type=f32)
        rows = slice(u * QB, (u + 1) * QB)
        attdq_ref[0, 0, rows] = diag_pick(att, heads).astype(jnp.bfloat16)
        dq = lax.dot_general(ds[u], keys[u], tn, preferred_element_type=f32)
        attdq_ref[0, 1, rows] = (diag_pick(dq, heads) * SCALE).astype(jnp.bfloat16)
    dk = [jnp.dot(ds[u], q_bd[u], preferred_element_type=f32) for u in every]
    dv = [jnp.dot(probs_low[u], g_bd[u], preferred_element_type=f32) for u in every]
    for u in every:
        for s in range(8):
            dk_acc[slots[u][s]] += dk[u][s * QB : (s + 1) * QB]
            dv_acc[slots[u][s]] += dv[u][s * QB : (s + 1) * QB]

    @pl.when(i == pl.num_programs(0) - 1)
    def _():
        for j, acc in ((0, dk_acc), (1, dv_acc)):
            for d in range(GROUP):
                start = reach + d * shard
                own_ref[d, j] = acc[start : start + shard]
            for e in range(4):
                start = e * shard if e < 2 else own + e * shard
                far_ref[e, j] = acc[start : start + shard].astype(jnp.bfloat16)


def attend(slots, usable, kv_pieces, kv_far, qg_pieces, reach, shard):
    width = kv_pieces[0].shape[-1]
    own = GROUP * shard
    win = own + 2 * reach
    bf16, f32 = jnp.bfloat16, jnp.float32
    anywhere = pl.BlockSpec(memory_space=pl.ANY)

    def whole(n):
        return pl.BlockSpec((n, 2, shard, QB, width), lambda i, *_: (0,) * 5)

    return pl.pallas_call(
        functools.partial(attend_kernel, reach=reach, shard=shard),
        grid_spec=pltpu.PrefetchScalarGridSpec(
            num_scalar_prefetch=2,
            grid=(own // UNROLL,),
            in_specs=[anywhere] * (2 * GROUP + 2),
            out_specs=[
                pl.BlockSpec(
                    (1, 2, UNROLL * QB, width),
                    lambda i, *_: (i // (shard // UNROLL), 0, i % (shard // UNROLL), 0),
                ),
                whole(GROUP),
                whole(4),
            ],
            scratch_shapes=[
                pltpu.VMEM((2, win, QB, width), bf16),
                pltpu.VMEM((2, own, QB, width), bf16),
                pltpu.VMEM((win, QB, width), f32),
                pltpu.VMEM((win, QB, width), f32),
                pltpu.SemaphoreType.DMA((2 * GROUP + 4,)),
            ],
        ),
        out_shape=[
            jax.ShapeDtypeStruct((GROUP, 2, shard * QB, width), bf16),
            jax.ShapeDtypeStruct((GROUP, 2, shard, QB, width), f32),
            jax.ShapeDtypeStruct((4, 2, shard, QB, width), bf16),
        ],
        cost_estimate=pl.CostEstimate(
            flops=120 * own * 8 * QB * width * width, bytes_accessed=16 << 20, transcendentals=own * 8 * QB * width
        ),
        compiler_params=pltpu.CompilerParams(dimension_semantics=("arbitrary",)),
        name="attend",
    )(slots, usable, *kv_pieces, *kv_far, *qg_pieces)


def lay_kernel(member_ref, *refs):
    per = len(refs) - 4
    pieces, outs = refs[:per], refs[per:]
    width = pieces[0].shape[-1]
    member = member_ref[0]
    at = 0
    for phase in range(PHASES):
        for pair in range(2):
            for d in range(GROUP):
                piece = pieces[at]
                at += 1
                start = pl.multiple_of(((member ^ d) * PHASES + phase) * width, width)
                for j in range(2):
                    value = piece[0, j] if d == 0 else piece[j]
                    outs[2 * pair + j][:, pl.ds(start, width)] = value


def lay(member, pieces, tokens, model, rows=128):
    in_specs = []
    for n, piece in enumerate(pieces):
        width = piece.shape[-1]
        if n % GROUP == 0:
            in_specs.append(pl.BlockSpec((1, 2, rows, width), lambda r, *_: (0, 0, r, 0)))
        else:
            in_specs.append(pl.BlockSpec((2, rows, width), lambda r, *_: (0, r, 0)))
    return pl.pallas_call(
        lay_kernel,
        grid_spec=pltpu.PrefetchScalarGridSpec(
            num_scalar_prefetch=1,
            grid=(tokens // rows,),
            in_specs=in_specs,
            out_specs=[pl.BlockSpec((rows, model), lambda r, *_: (r, 0))] * 4,
        ),
        out_shape=[jax.ShapeDtypeStruct((tokens, model), jnp.bfloat16)] * 4,
        name="lay",
    )(member, *pieces)


def on_device(queries, keys, values, out_grad, pattern):
    tokens, model = queries.shape
    shard = tokens // QB
    count = lax.axis_size("seq")
    me = lax.axis_index("seq")
    member = me % GROUP
    high, low = member // 2, member % 2
    cols = model // GROUP
    width = cols // PHASES
    reach = 2 * shard
    own = GROUP * shard

    def swap(value, d):
        return lax.ppermute(value, "seq", [(s, s ^ d) for s in range(count)])

    def hop(value, step):
        pairs = [(s, s + step) for s in range(max(0, -step), min(count, count - step))]
        return lax.ppermute(value, "seq", pairs)

    level_pattern = jnp.stack([pattern] + [swap(pattern, d) for d in range(1, GROUP)])
    place = jnp.arange(GROUP, dtype=jnp.int32)[:, None]
    local = ((place ^ member) * shard + jnp.arange(shard, dtype=jnp.int32)).reshape(own, 1)
    near = jnp.broadcast_to(jnp.array([-2, -1, 0, 1], dtype=jnp.int32), (own, 4))
    target = local + jnp.concatenate([near, level_pattern.reshape(own, 4)], axis=1)
    in_shard = target % shard
    level_shard = target // shard
    inside = (level_shard >= 0) & (level_shard < GROUP)
    held = jnp.where(
        inside,
        2 + (level_shard ^ member),
        jnp.where(level_shard < 0, (level_shard + 2) ^ low, 2 + GROUP + ((level_shard - GROUP) ^ low)),
    )
    slots = held * shard + in_shard
    target = target + (me // GROUP) * own
    usable = ((target >= 0) & (target < count * shard)).astype(jnp.int32)

    def cut(arrays, d, phase):
        start = (member ^ d) * cols + phase * width
        return jnp.stack([lax.dynamic_slice_in_dim(a, start, width, 1) for a in arrays])

    def bring(arrays, phase):
        return [cut(arrays, 0, phase)] + [swap(cut(arrays, d, phase), d) for d in range(1, GROUP)]

    kvs = [bring((keys, values), phase) for phase in range(PHASES)]
    qgs = [bring((queries, out_grad), phase) for phase in range(PHASES)]
    fars = []
    for kv in kvs:
        near_pair, cross_pair = jnp.stack(kv[:2]), jnp.stack(kv[2:])
        upper = jnp.where(high == 1, near_pair, cross_pair)
        lower = jnp.where(high == 1, cross_pair, near_pair)
        fars.append((hop(upper, GROUP), hop(lower, -GROUP)))

    blocked = (2, shard, QB, width)
    pieces = []
    for phase in range(PHASES):
        attdq, own_grads, far_grads = attend(
            slots,
            usable,
            [p.reshape(blocked) for p in kvs[phase]],
            [f.reshape((2,) + blocked) for f in fars[phase]],
            [p.reshape(blocked) for p in qgs[phase]],
            reach,
            shard,
        )
        far_grads = far_grads.reshape(4, 2, tokens, width)
        own_grads = own_grads.reshape(GROUP, 2, tokens, width)
        for_upper = hop(far_grads[:2], -GROUP)
        for_lower = hop(far_grads[2:], GROUP)
        pieces += [attdq] + [swap(attdq[d], d) for d in range(1, GROUP)]
        near_add = jnp.where(high == 1, for_upper, for_lower)
        cross_add = jnp.where(high == 1, for_lower, for_upper)
        add = jnp.concatenate([near_add, cross_add]).astype(jnp.float32)
        grads = (own_grads + add).astype(jnp.bfloat16)
        pieces += [grads] + [swap(grads[d], d) for d in range(1, GROUP)]
    return tuple(lay(member.reshape(1), pieces, tokens, model))


def solution(mesh):
    spec = P(("dp", "seq"), None)
    return jax.shard_map(
        on_device,
        mesh=mesh,
        in_specs=(spec,) * 5,
        out_specs=(spec,) * 4,
        check_vma=False,
    )
```

```python
import functools

import jax
import jax.numpy as jnp
from jax import lax
from jax.experimental import pallas as pl
from jax.experimental.pallas import tpu as pltpu
from jax.sharding import PartitionSpec as P

HEAD = 64
QB = 64
GROUP = 4
PHASES = 1
UNROLL = 4
NEG = -1e30
SCALE = HEAD ** (-0.5)


def diag_rows(block, heads):
    tiled = jnp.concatenate([block] * heads, axis=0)
    row = lax.broadcasted_iota(jnp.int32, tiled.shape, 0) // QB
    col = lax.broadcasted_iota(jnp.int32, tiled.shape, 1) // HEAD
    return jnp.where(row == col, tiled, jnp.zeros_like(tiled))


def diag_pick(full, heads):
    col = lax.broadcasted_iota(jnp.int32, (QB, heads * HEAD), 1) // HEAD
    out = full[:QB]
    for h in range(1, heads):
        out = jnp.where(col == h, full[h * QB : (h + 1) * QB], out)
    return out


def attend_kernel(*refs, reach, shard):
    slot_ref, usable_ref = refs[:2]
    kv_pieces, kv_far, qg_pieces = refs[2 : 2 + GROUP], refs[2 + GROUP : 4 + GROUP], refs[4 + GROUP : 4 + 2 * GROUP]
    attdq_ref, own_ref, far_ref, kv_win, qg_win, dk_acc, dv_acc, sems = refs[4 + 2 * GROUP :]
    i = pl.program_id(0)
    width = kv_win.shape[-1]
    heads = width // HEAD
    own = GROUP * shard

    @pl.when(i == 0)
    def _():
        copies = []

        def bring(src, dst):
            copy = pltpu.make_async_copy(src, dst, sems.at[len(copies)])
            copy.start()
            copies.append(copy)

        for d in range(GROUP):
            bring(kv_pieces[d], kv_win.at[:, reach + d * shard : reach + (d + 1) * shard])
            bring(qg_pieces[d], qg_win.at[:, d * shard : (d + 1) * shard])
        for side, base in enumerate((0, reach + own)):
            for e in range(2):
                start = base + e * shard
                bring(kv_far[side].at[e], kv_win.at[:, start : start + shard])
        dk_acc[...] = jnp.zeros_like(dk_acc)
        dv_acc[...] = jnp.zeros_like(dv_acc)
        for copy in copies:
            copy.wait()

    nt = (((1,), (1,)), ((), ()))
    tn = (((0,), (0,)), ((), ()))
    f32 = jnp.float32
    every = range(UNROLL)
    blocks = [i * UNROLL + u for u in every]
    slots = [[slot_ref[b, s] for s in range(8)] for b in blocks]
    q_bd = [diag_rows(qg_win[0, b] * jnp.bfloat16(SCALE), heads) for b in blocks]
    g_bd = [diag_rows(qg_win[1, b], heads) for b in blocks]
    keys = [jnp.concatenate([kv_win[0, t] for t in slots[u]], axis=0) for u in every]
    vals = [jnp.concatenate([kv_win[1, t] for t in slots[u]], axis=0) for u in every]
    raw = [lax.dot_general(keys[u], q_bd[u], nt, preferred_element_type=f32) for u in every]
    grad_probs = [lax.dot_general(vals[u], g_bd[u], nt, preferred_element_type=f32) for u in every]
    probs_low, ds = [], []
    for u in every:
        parts = []
        for s in range(8):
            part = raw[u][s * QB : (s + 1) * QB]
            if s != 2:
                part = part + jnp.where(usable_ref[blocks[u], s] != 0, 0.0, NEG).astype(f32)
            if s == 0:
                within = lax.broadcasted_iota(jnp.int32, part.shape, 0)
                pos = lax.broadcasted_iota(jnp.int32, part.shape, 1) % QB
                part = jnp.where(within >= pos, part, NEG)
            parts.append(part)
        scores = jnp.concatenate(parts, axis=0)
        top = jnp.max(scores, axis=0, keepdims=True)
        lifted = jnp.exp(scores - top)
        inv = 1.0 / jnp.sum(lifted, axis=0, keepdims=True)
        probs = lifted * inv
        probs_low.append(probs.astype(jnp.bfloat16))
        dots = jnp.sum(probs * grad_probs[u], axis=0, keepdims=True)
        ds.append((probs * (grad_probs[u] - dots)).astype(jnp.bfloat16))
    for u in every:
        att = lax.dot_general(probs_low[u], vals[u], tn, preferred_element_type=f32)
        rows = slice(u * QB, (u + 1) * QB)
        attdq_ref[0, 0, rows] = diag_pick(att, heads).astype(jnp.bfloat16)
        dq = lax.dot_general(ds[u], keys[u], tn, preferred_element_type=f32)
        attdq_ref[0, 1, rows] = (diag_pick(dq, heads) * SCALE).astype(jnp.bfloat16)
    dk = [jnp.dot(ds[u], q_bd[u], preferred_element_type=f32) for u in every]
    dv = [jnp.dot(probs_low[u], g_bd[u], preferred_element_type=f32) for u in every]
    for u in every:
        for s in range(8):
            dk_acc[slots[u][s]] += dk[u][s * QB : (s + 1) * QB]
            dv_acc[slots[u][s]] += dv[u][s * QB : (s + 1) * QB]

    @pl.when(i == pl.num_programs(0) - 1)
    def _():
        for j, acc in ((0, dk_acc), (1, dv_acc)):
            for d in range(GROUP):
                start = reach + d * shard
                own_ref[d, j] = acc[start : start + shard]
            for e in range(4):
                start = e * shard if e < 2 else own + e * shard
                far_ref[e, j] = acc[start : start + shard].astype(jnp.bfloat16)


def attend(slots, usable, kv_pieces, kv_far, qg_pieces, reach, shard):
    width = kv_pieces[0].shape[-1]
    own = GROUP * shard
    win = own + 2 * reach
    bf16, f32 = jnp.bfloat16, jnp.float32
    anywhere = pl.BlockSpec(memory_space=pl.ANY)

    def whole(n):
        return pl.BlockSpec((n, 2, shard, QB, width), lambda i, *_: (0,) * 5)

    return pl.pallas_call(
        functools.partial(attend_kernel, reach=reach, shard=shard),
        grid_spec=pltpu.PrefetchScalarGridSpec(
            num_scalar_prefetch=2,
            grid=(own // UNROLL,),
            in_specs=[anywhere] * (2 * GROUP + 2),
            out_specs=[
                pl.BlockSpec(
                    (1, 2, UNROLL * QB, width),
                    lambda i, *_: (i // (shard // UNROLL), 0, i % (shard // UNROLL), 0),
                ),
                whole(GROUP),
                whole(4),
            ],
            scratch_shapes=[
                pltpu.VMEM((2, win, QB, width), bf16),
                pltpu.VMEM((2, own, QB, width), bf16),
                pltpu.VMEM((win, QB, width), f32),
                pltpu.VMEM((win, QB, width), f32),
                pltpu.SemaphoreType.DMA((2 * GROUP + 4,)),
            ],
        ),
        out_shape=[
            jax.ShapeDtypeStruct((GROUP, 2, shard * QB, width), bf16),
            jax.ShapeDtypeStruct((GROUP, 2, shard, QB, width), f32),
            jax.ShapeDtypeStruct((4, 2, shard, QB, width), bf16),
        ],
        cost_estimate=pl.CostEstimate(
            flops=120 * own * 8 * QB * width * width, bytes_accessed=16 << 20, transcendentals=own * 8 * QB * width
        ),
        compiler_params=pltpu.CompilerParams(dimension_semantics=("arbitrary",)),
        name="attend",
    )(slots, usable, *kv_pieces, *kv_far, *qg_pieces)


def lay_kernel(member_ref, *refs):
    per = len(refs) - 4
    pieces, outs = refs[:per], refs[per:]
    width = pieces[0].shape[-1]
    member = member_ref[0]
    at = 0
    for phase in range(PHASES):
        for pair in range(2):
            for d in range(GROUP):
                piece = pieces[at]
                at += 1
                start = pl.multiple_of(((member ^ d) * PHASES + phase) * width, width)
                for j in range(2):
                    value = piece[0, j] if d == 0 else piece[j]
                    outs[2 * pair + j][:, pl.ds(start, width)] = value


def lay(member, pieces, tokens, model, rows=128):
    in_specs = []
    for n, piece in enumerate(pieces):
        width = piece.shape[-1]
        if n % GROUP == 0:
            in_specs.append(pl.BlockSpec((1, 2, rows, width), lambda r, *_: (0, 0, r, 0)))
        else:
            in_specs.append(pl.BlockSpec((2, rows, width), lambda r, *_: (0, r, 0)))
    return pl.pallas_call(
        lay_kernel,
        grid_spec=pltpu.PrefetchScalarGridSpec(
            num_scalar_prefetch=1,
            grid=(tokens // rows,),
            in_specs=in_specs,
            out_specs=[pl.BlockSpec((rows, model), lambda r, *_: (r, 0))] * 4,
        ),
        out_shape=[jax.ShapeDtypeStruct((tokens, model), jnp.bfloat16)] * 4,
        name="lay",
    )(member, *pieces)


def on_device(queries, keys, values, out_grad, pattern):
    tokens, model = queries.shape
    shard = tokens // QB
    count = lax.axis_size("seq")
    me = lax.axis_index("seq")
    member = me % GROUP
    high, low = member // 2, member % 2
    cols = model // GROUP
    width = cols // PHASES
    reach = 2 * shard
    own = GROUP * shard

    def swap(value, d):
        return lax.ppermute(value, "seq", [(s, s ^ d) for s in range(count)])

    def hop(value, step):
        pairs = [(s, s + step) for s in range(max(0, -step), min(count, count - step))]
        return lax.ppermute(value, "seq", pairs)

    level_pattern = jnp.stack([pattern] + [swap(pattern, d) for d in range(1, GROUP)])
    place = jnp.arange(GROUP, dtype=jnp.int32)[:, None]
    local = ((place ^ member) * shard + jnp.arange(shard, dtype=jnp.int32)).reshape(own, 1)
    near = jnp.broadcast_to(jnp.array([-2, -1, 0, 1], dtype=jnp.int32), (own, 4))
    target = local + jnp.concatenate([near, level_pattern.reshape(own, 4)], axis=1)
    in_shard = target % shard
    level_shard = target // shard
    inside = (level_shard >= 0) & (level_shard < GROUP)
    held = jnp.where(
        inside,
        2 + (level_shard ^ member),
        jnp.where(level_shard < 0, (level_shard + 2) ^ low, 2 + GROUP + ((level_shard - GROUP) ^ low)),
    )
    slots = held * shard + in_shard
    target = target + (me // GROUP) * own
    usable = ((target >= 0) & (target < count * shard)).astype(jnp.int32)

    def cut(arrays, d, phase):
        start = (member ^ d) * cols + phase * width
        return jnp.stack([lax.dynamic_slice_in_dim(a, start, width, 1) for a in arrays])

    def bring(arrays, phase):
        return [cut(arrays, 0, phase)] + [swap(cut(arrays, d, phase), d) for d in range(1, GROUP)]

    kvs = [bring((keys, values), phase) for phase in range(PHASES)]
    qgs = [bring((queries, out_grad), phase) for phase in range(PHASES)]
    fars = []
    for kv in kvs:
        near_pair, cross_pair = jnp.stack(kv[:2]), jnp.stack(kv[2:])
        upper = jnp.where(high == 1, near_pair, cross_pair)
        lower = jnp.where(high == 1, cross_pair, near_pair)
        fars.append((hop(upper, GROUP), hop(lower, -GROUP)))

    blocked = (2, shard, QB, width)
    pieces = []
    for phase in range(PHASES):
        attdq, own_grads, far_grads = attend(
            slots,
            usable,
            [p.reshape(blocked) for p in kvs[phase]],
            [f.reshape((2,) + blocked) for f in fars[phase]],
            [p.reshape(blocked) for p in qgs[phase]],
            reach,
            shard,
        )
        far_grads = far_grads.reshape(4, 2, tokens, width)
        own_grads = own_grads.reshape(GROUP, 2, tokens, width)
        for_upper = hop(far_grads[:2], -GROUP)
        for_lower = hop(far_grads[2:], GROUP)
        pieces += [attdq] + [swap(attdq[d], d) for d in range(1, GROUP)]
        near_add = jnp.where(high == 1, for_upper, for_lower)
        cross_add = jnp.where(high == 1, for_lower, for_upper)
        add = jnp.concatenate([near_add, cross_add]).astype(jnp.float32)
        grads = (own_grads + add).astype(jnp.bfloat16)
        pieces += [grads] + [swap(grads[d], d) for d in range(1, GROUP)]
    return tuple(lay(member.reshape(1), pieces, tokens, model))


def solution(mesh):
    spec = P(("dp", "seq"), None)
    return jax.shard_map(
        on_device,
        mesh=mesh,
        in_specs=(spec,) * 5,
        out_specs=(spec,) * 4,
        check_vma=False,
    )
```
